32 devices in a mesh: win: 2 (over y), bl: 4 (over x, core), freq: 4 (over z).
Axes of the slice: x: 2, y: 2, z: 4, core: 2. Of those that a mesh axis runs over, the one named last changes fastest.
Arguments:
- vis: bfloat16 [64, 1536, 2, 512], P('bl', 'freq', None, 'win'), parts along dimension 3, may hold values from -6 to 6
- flags: int32 [64, 1536], P('bl', 'freq'), may hold values 0 or 1
- band: int32 [64], P('bl'), may hold values from 0 to 7
- group_id: int32 [64], P('bl'), may hold values from 0 to 7, as said below
Outputs:
- averaged: bfloat16 [8, 2, 512, 1536], P('bl', None, ('win', 'freq')), parts along dimension 2
The draws below stay inside these ranges and needn't reach their ends.
There are 2 independent parts, one for each index of `win`. The reference program is written for one: setup_inputs(seed, part) draws one part's arguments, and reference() takes and returns one part's arrays. A program takes and returns all parts, laid end to end along the dimension named above; an argument that names none is the same for every part. Nothing has to cross between parts.
Inputs may be any that keep to these rules, and one draw needn't show every extreme that they name: `group_id`: of each aligned block of 16 baselines (those of one index of bl), at most 8 belong to the groups of one owner; in every draw one owner receives exactly 8 from every block.
All inputs are finite; a program needn't handle non-finite values. No bound on the sum of `flags` on one device may be relied on, other than what follows from the above.
Results may differ from the reference program's by a relative error of at most 0.0071.
Values may be sent and summed in bfloat16 or wider, within the bound.
A program may use at most 64 MiB of HBM per device.

```python
import math
import jax
import jax.numpy as jnp
from jax import lax

CH = 1536
DELAYS = 128
NBAND = 8
TIME = 256
B_BL = 16
GPO = 2
CAP = 8
B = 64
NG = 8
N_BL = 4


def draw_group_id(key, part):
    key_busy, key_rest, key_order, key_local = jax.random.split(jax.random.fold_in(key, 17), 4)
    busiest = jax.random.randint(key_busy, (), 0, N_BL)
    others = jax.random.randint(key_rest, (N_BL, B_BL - CAP), 0, N_BL - 1)
    others = others + (others >= busiest).astype(jnp.int32)
    owner_of = jnp.concatenate([jnp.full((N_BL, CAP), 0, jnp.int32) + busiest, others], axis=1)
    order_keys = jax.random.split(key_order, N_BL)
    orders = jax.vmap(lambda sub_key: jax.random.permutation(sub_key, B_BL))(order_keys)
    owner_of = jnp.take_along_axis(owner_of, orders.astype(jnp.int32), axis=1)
    local_ids = jax.random.randint(key_local, (N_BL, B_BL), 0, GPO)
    return (owner_of * GPO + local_ids).reshape(N_BL * B_BL).astype(jnp.int32)


def plant(entries, rng, least, top_value):
    extent = entries.shape
    index_at = [jax.random.randint(jax.random.fold_in(rng, axis), (), 0, extent[axis]) for axis in range(len(extent))]
    entries = entries.at[tuple(index_at)].set(least)
    longest = extent.index(max(extent))
    index_at[longest] = (index_at[longest] + 1) % extent[longest]
    return entries.at[tuple(index_at)].set(top_value)


def block_levels(rng, dims, cuts, smallest, top_value):
    level, own = 1.0, jax.random.fold_in(rng, 6)
    for dim, shards_of in cuts:
        heights = jnp.exp(jax.random.uniform(jax.random.fold_in(own, dim), (shards_of,), jnp.float32, smallest / len(cuts), top_value / len(cuts)))
        level = level * jnp.repeat(heights, dims[dim] // shards_of).reshape([-1 if axis == dim else 1 for axis in range(len(dims))])
    return level


def scatter_about(key, dims, width, most, cuts=(), kind=jnp.bfloat16):
    array = width * jax.random.normal(key, dims, jnp.float32)
    if cuts:
        array = array * block_levels(key, dims, cuts, -0.22, 0.18)
    return jnp.clip(array, -most, most).astype(kind)


def setup_inputs(seed: int = 0, part: int = 0) -> dict:
    streams_of = jax.random.split(jax.random.key(seed), 5)
    part_keys = jax.random.split(jax.random.fold_in(streams_of[4], part), 5)
    vis = scatter_about(part_keys[0], (B, CH, 2, TIME), 1.0, 6.0, ((0, 4), (1, 4)))
    flags = plant((jax.random.randint(streams_of[1], (B, CH), 0, 8) < 1).astype(jnp.int32), jax.random.fold_in(streams_of[1], 1), 0, 1)
    band = plant(jax.random.randint(streams_of[2], (B,), 0, NBAND), jax.random.fold_in(streams_of[2], 1), 0, NBAND - 1).astype(jnp.int32)
    group_id = draw_group_id(jax.random.fold_in(streams_of[4], 71), part)
    return dict(vis=vis, flags=flags, band=band, group_id=group_id)


def fourier_tables(length):
    sample_index = jnp.arange(length, dtype=jnp.int32)
    phase_index = sample_index[:, None] * sample_index[None, :] % length
    angles = phase_index.astype(jnp.float32) * (2.0 * math.pi / length)
    cosine = jnp.cos(angles)
    sine_table = jnp.sin(angles)
    forward = jnp.concatenate([jnp.concatenate([cosine, -sine_table], 1), jnp.concatenate([sine_table, cosine], 1)], 0)
    inverse = jnp.concatenate([jnp.concatenate([cosine, sine_table], 1), jnp.concatenate([-sine_table, cosine], 1)], 0)
    return (forward.astype(jnp.bfloat16), inverse.astype(jnp.bfloat16))

def band_response(band, length, band_count):
    mode_index = jnp.arange(length, dtype=jnp.int32)
    signed_modes = (mode_index - length * (mode_index >= length // 2).astype(jnp.int32)).astype(jnp.float32)
    center = (band.astype(jnp.float32) - (band_count - 1) / 2.0) * (length / (4.0 * band_count))
    band_width = length / 32.0
    offset_ratio = (signed_modes[None, :] - center[:, None]) / band_width
    single = (0.15 + 0.85 / (1.0 + offset_ratio ** 4)) / length
    return jnp.concatenate([single, single], 1)

def make_basis(channels, modes):
    channel_index = jnp.arange(channels, dtype=jnp.int32)
    order_index = jnp.arange(modes, dtype=jnp.int32)
    phase_index = order_index[None, :] * (2 * channel_index[:, None] + 1) % (4 * channels)
    return jnp.cos(phase_index.astype(jnp.float32) * (math.pi / (2 * channels))).astype(jnp.bfloat16)

def reference(vis, flags, band, group_id):
    forward, inverse = fourier_tables(TIME)
    response = band_response(band, TIME, NBAND)

    def fringe_block(inputs):
        block, block_response = inputs
        flat_rows = block.reshape(B_BL * CH, 2 * TIME)
        spectra = jnp.dot(flat_rows.astype(jnp.float32), forward.astype(jnp.float32), preferred_element_type=jnp.float32).reshape(B_BL, CH, 2 * TIME)
        spectra = (spectra * block_response[:, None, :]).astype(jnp.bfloat16)
        result = jnp.dot(spectra.reshape(B_BL * CH, 2 * TIME).astype(jnp.float32), inverse.astype(jnp.float32), preferred_element_type=jnp.float32)
        return result.astype(jnp.bfloat16).reshape(B_BL, CH, 2, TIME)
    fringe = lax.map(fringe_block, (vis.reshape(N_BL, B_BL, CH, 2, TIME), response.reshape(N_BL, B_BL, 2 * TIME)))
    fringe = fringe.reshape(B, CH, 2, TIME)
    weight = 1.0 - flags.astype(jnp.float32)
    delay_basis = make_basis(CH, DELAYS)
    basis_wide = delay_basis.astype(jnp.float32)
    ridge_scale = CH / 64.0
    select = group_id[None, :] == jnp.arange(NG, dtype=jnp.int32)[:, None]
    counts = jnp.sum(select.astype(jnp.float32), 1)

    def clean_one(sums, inputs):
        column, weight_row, group_index = inputs
        normal = jnp.dot(basis_wide.T * weight_row[None, :], basis_wide, precision=lax.Precision.HIGHEST)
        normal = normal + ridge_scale * jnp.eye(DELAYS, dtype=jnp.float32)
        factor = jnp.linalg.cholesky(normal)
        masked = column * weight_row[:, None, None].astype(jnp.bfloat16)
        projected = jnp.einsum('crt,ck->krt', masked.astype(jnp.float32), basis_wide).reshape(DELAYS, 2 * TIME)
        half_solved = lax.linalg.triangular_solve(factor, projected, left_side=True, lower=True)
        coefficients = lax.linalg.triangular_solve(factor, half_solved, left_side=True, lower=True, transpose_a=True)
        coefficients = coefficients.reshape(DELAYS, 2, TIME)
        fitted = jnp.einsum('krt,ck->rtc', coefficients, basis_wide, precision=lax.Precision.HIGHEST)
        cleaned = (weight_row[None, None, :] * (jnp.transpose(column, (1, 2, 0)).astype(jnp.float32) - fitted)).astype(jnp.bfloat16)
        zero_index = jnp.zeros((), jnp.int32)
        start = (group_index.astype(jnp.int32), zero_index, zero_index, zero_index)
        current = lax.dynamic_slice(sums, start, (1, 2, TIME, CH))
        sums = lax.dynamic_update_slice(sums, current + cleaned.astype(jnp.float32)[None], start)
        return (sums, None)
    initial = jnp.zeros((NG, 2, TIME, CH), jnp.float32)
    group_sums, unused = lax.scan(clean_one, initial, (fringe, weight, group_id))
    return (group_sums / jnp.maximum(counts, 1.0)[:, None, None, None]).astype(jnp.bfloat16)
```

```python
import functools
import math

import jax
import jax.numpy as jnp
from jax import lax
from jax.experimental import pallas as pl
from jax.experimental.pallas import tpu as pltpu
from jax.sharding import PartitionSpec as P

CH = 1536
DELAYS = 128
NBAND = 8
GPO = 2
CAP = 8


def fourier_tables(length):
    sample_index = jnp.arange(length, dtype=jnp.int32)
    phase_index = sample_index[:, None] * sample_index[None, :] % length
    angles = phase_index.astype(jnp.float32) * (2.0 * math.pi / length)
    cosine = jnp.cos(angles)
    sine_table = jnp.sin(angles)
    forward = jnp.concatenate(
        [jnp.concatenate([cosine, -sine_table], 1), jnp.concatenate([sine_table, cosine], 1)], 0
    )
    return forward.astype(jnp.bfloat16)


def band_response(band, length, band_count):
    mode_index = jnp.arange(length, dtype=jnp.int32)
    signed_modes = (mode_index - length * (mode_index >= length // 2).astype(jnp.int32)).astype(
        jnp.float32
    )
    center = (band.astype(jnp.float32) - (band_count - 1) / 2.0) * (length / (4.0 * band_count))
    band_width = length / 32.0
    offset_ratio = (signed_modes[None, :] - center[:, None]) / band_width
    single = (0.15 + 0.85 / (1.0 + offset_ratio**4)) / length
    return jnp.concatenate([single, single], 1)


def make_basis(channels, modes):
    channel_index = jnp.arange(channels, dtype=jnp.int32)
    order_index = jnp.arange(modes, dtype=jnp.int32)
    phase_index = order_index[None, :] * (2 * channel_index[:, None] + 1) % (4 * channels)
    return jnp.cos(phase_index.astype(jnp.float32) * (math.pi / (2 * channels))).astype(
        jnp.bfloat16
    )


NT = (((1,), (1,)), ((), ()))
BIG = 48 * 1024 * 1024


def dot32(left, right):
    return jnp.dot(left, right, preferred_element_type=jnp.float32)


def halves(value):
    high = value.astype(jnp.bfloat16)
    return high, (value - high.astype(jnp.float32)).astype(jnp.bfloat16)


def dot_split(left, right):
    left_high, left_low = left
    right_high, right_low = right
    return dot32(left_high, right_high) + (
        dot32(left_high, right_low) + dot32(left_low, right_high)
    )


def filter_kernel(shards, re_ref, im_ref, fwd_ref, inv_ref, resp_ref, weight_ref, basis_ref,
                  fringe_ref, proj_ref):
    half = re_ref.shape[2]
    spectra = dot32(re_ref[0], fwd_ref[:half]) + dot32(im_ref[0], fwd_ref[half:])
    spectra = (spectra * resp_ref[0]).astype(jnp.bfloat16)
    fringe = lax.dot_general(inv_ref[...], spectra, NT, preferred_element_type=jnp.float32)
    fringe = (fringe * weight_ref[0]).astype(jnp.bfloat16)
    fringe_ref[0] = fringe
    projected = dot32(fringe, basis_ref[...])
    proj_ref[:, 0] = projected.reshape(shards, -1, projected.shape[1]).astype(jnp.bfloat16)


def inverse_kernel(batch, ridge, scales, start, weight_ref, basis_ref, basis_t_ref, out_ref):
    modes = out_ref.shape[1]
    eye = (
        lax.broadcasted_iota(jnp.int32, (modes, modes), 0)
        == lax.broadcasted_iota(jnp.int32, (modes, modes), 1)
    ).astype(jnp.float32)
    normals = [
        dot32(basis_t_ref[...] * weight_ref[i], basis_ref[...]) + ridge * eye for i in range(batch)
    ]
    first = scales[0]
    guess = [first * (2.0 * start * eye - start * start * normal) for normal in normals]
    normals = [halves(normal) for normal in normals]
    for scale in scales[1:]:
        guess_parts = [halves(value) for value in guess]
        product = [dot_split(n, g) for n, g in zip(normals, guess_parts)]
        change = [halves(2.0 * eye - value) for value in product]
        guess = [scale * dot_split(g, c) for g, c in zip(guess_parts, change)]
    for i in range(batch):
        out_ref[i] = guess[i]


def solve_kernel(batch, recv_ref, inverse_ref, out_ref):
    for i in range(batch):
        total = jnp.sum(recv_ref[:, i].astype(jnp.float32), axis=0)
        out_ref[i] = dot_split(halves(total), halves(inverse_ref[i])).astype(jnp.bfloat16)


def clean_kernel(ids_ref, fringe_ref, coef_ref, basis_t_ref, weight_ref, out_ref, total_ref):
    item = pl.program_id(0)

    @pl.when(item == 0)
    def _():
        total_ref[...] = jnp.zeros_like(total_ref)

    coef = coef_ref[:, 0].astype(jnp.float32)
    coef = coef.reshape(-1, coef.shape[2]).astype(jnp.bfloat16)
    fitted = dot32(coef, basis_t_ref[...]) * weight_ref[0]
    cleaned = fringe_ref[0].astype(jnp.float32) - fitted
    group = ids_ref[item]
    total_ref[group] += cleaned

    @pl.when(item == pl.num_programs(0) - 1)
    def _():
        out_ref[...] = total_ref[...].astype(jnp.bfloat16)


def newton_scales(low, high):
    scales = []
    value = (high + low) / (high - low)
    while True:
        doubled = 2.0 * value * value
        scales.append(doubled / (doubled - 1.0))
        value = doubled - 1.0
        if value > 1e6:
            return scales


def full(shape):
    return pl.BlockSpec(shape, lambda i, *rest: (0,) * len(shape))


def lead(shape):
    return pl.BlockSpec(shape, lambda i, *rest: (i,) + (0,) * (len(shape) - 1))


def second(shape):
    return pl.BlockSpec(shape, lambda i, *rest: (0, i) + (0,) * (len(shape) - 2))


def per_device(vis, flags, band, group_id):
    items, chan, _, length = vis.shape
    both = 2 * length
    shards = lax.axis_size("freq")
    owners = lax.axis_size("bl")
    groups = GPO * owners
    time_local = length // shards
    rows = 2 * time_local
    bf16, f32 = jnp.bfloat16, jnp.float32

    forward = fourier_tables(length)
    inverse_t = forward.reshape(2, shards, time_local, both)
    inverse_t = jnp.transpose(inverse_t, (1, 0, 2, 3)).reshape(both, both)
    response = band_response(band, length, NBAND).reshape(items, 1, both)
    basis = make_basis(CH, DELAYS)
    basis_t = basis.T
    basis_local = lax.dynamic_slice_in_dim(basis, lax.axis_index("freq") * chan, chan, 0)
    weight = 1.0 - flags.astype(f32)
    weight_rows = weight.reshape(items, 1, chan)
    weight_full = lax.all_gather(weight.astype(bf16), "freq", axis=1, tiled=True)
    weight_full = weight_full.reshape(items, 1, CH)

    fringe, projected = pl.pallas_call(
        functools.partial(filter_kernel, shards),
        grid=(items,),
        in_specs=[
            lead((1, chan, length)), lead((1, chan, length)), full((both, both)),
            full((both, both)), lead((1, 1, both)), lead((1, 1, chan)), full((chan, DELAYS)),
        ],
        out_specs=[lead((1, both, chan)), second((shards, 1, rows, DELAYS))],
        out_shape=[
            jax.ShapeDtypeStruct((items, both, chan), bf16),
            jax.ShapeDtypeStruct((shards, items, rows, DELAYS), bf16),
        ],
        compiler_params=pltpu.CompilerParams(vmem_limit_bytes=BIG),
        cost_estimate=pl.CostEstimate(
            flops=4 * items * chan * both * both, bytes_accessed=4 * items * chan * both,
            transcendentals=0,
        ),
    )(vis[:, :, 0, :], vis[:, :, 1, :], forward, inverse_t, response, weight_rows, basis_local)

    ridge = CH / 64.0
    high = ridge + 1.05 * CH
    batch = 4 if items % 4 == 0 else 1
    inverse = pl.pallas_call(
        functools.partial(
            inverse_kernel, batch, ridge, newton_scales(ridge, high), 2.0 / (ridge + high)
        ),
        grid=(items // batch,),
        in_specs=[lead((batch, 1, CH)), full((CH, DELAYS)), full((DELAYS, CH))],
        out_specs=lead((batch, DELAYS, DELAYS)),
        out_shape=jax.ShapeDtypeStruct((items, DELAYS, DELAYS), f32),
        compiler_params=pltpu.CompilerParams(vmem_limit_bytes=BIG),
        cost_estimate=pl.CostEstimate(
            flops=20_000_000_000, bytes_accessed=4 * items * DELAYS * DELAYS, transcendentals=0
        ),
    )(weight_full, basis, basis_t)

    received = lax.all_to_all(projected, "freq", split_axis=0, concat_axis=0, tiled=True)
    coefficients = pl.pallas_call(
        functools.partial(solve_kernel, batch),
        grid=(items // batch,),
        in_specs=[second((shards, batch, rows, DELAYS)), lead((batch, DELAYS, DELAYS))],
        out_specs=lead((batch, rows, DELAYS)),
        out_shape=jax.ShapeDtypeStruct((items, rows, DELAYS), bf16),
        compiler_params=pltpu.CompilerParams(vmem_limit_bytes=BIG),
    )(received, inverse)
    coefficients = lax.all_gather(coefficients, "freq")

    sums = pl.pallas_call(
        clean_kernel,
        grid_spec=pltpu.PrefetchScalarGridSpec(
            num_scalar_prefetch=1,
            grid=(items,),
            in_specs=[
                lead((1, both, chan)), second((shards, 1, rows, DELAYS)), full((DELAYS, chan)),
                lead((1, 1, chan)),
            ],
            out_specs=full((groups, both, chan)),
            scratch_shapes=[pltpu.VMEM((groups, both, chan), f32)],
        ),
        out_shape=jax.ShapeDtypeStruct((groups, both, chan), bf16),
        compiler_params=pltpu.CompilerParams(vmem_limit_bytes=BIG),
    )(group_id, fringe, coefficients, basis_local.T, weight_rows)

    arrived = lax.all_to_all(sums, "bl", split_axis=0, concat_axis=0, tiled=True)
    ids = lax.all_gather(group_id, "bl", tiled=True) - lax.axis_index("bl") * GPO
    hits = (ids[None, :] == jnp.arange(GPO, dtype=jnp.int32)[:, None]).astype(f32)
    counts = jnp.maximum(jnp.sum(hits, 1), 1.0)
    total = jnp.sum(arrived.reshape(owners, GPO, both, chan).astype(f32), 0)
    mean = (total / counts[:, None, None]).astype(bf16).reshape(GPO, shards, rows, chan)
    swapped = lax.all_to_all(
        jnp.transpose(mean, (1, 0, 2, 3)), "freq", split_axis=0, concat_axis=0, tiled=True
    )
    averaged = jnp.transpose(swapped, (1, 2, 0, 3))
    return averaged.reshape(GPO, 2, time_local, CH)


def solution(mesh):
    in_specs = (P("bl", "freq", None, "win"), P("bl", "freq"), P("bl"), P("bl"))
    out_specs = P("bl", None, ("win", "freq"), None)
    return jax.shard_map(
        per_device, mesh=mesh, in_specs=in_specs, out_specs=out_specs, check_vma=False
    )
```

```python
import functools
import math

import jax
import jax.numpy as jnp
import numpy as np
from jax import lax
from jax.experimental import pallas as pl
from jax.experimental.pallas import tpu as pltpu
from jax.sharding import PartitionSpec as P

CH = 1536
DELAYS = 128
NBAND = 8
GPO = 2
CAP = 8


def fourier_tables(length):
    sample_index = np.arange(length, dtype=np.int32)
    phase_index = sample_index[:, None] * sample_index[None, :] % length
    angles = phase_index.astype(np.float32) * np.float32(2.0 * math.pi / length)
    cosine = np.cos(angles)
    sine_table = np.sin(angles)
    forward = np.concatenate(
        [np.concatenate([cosine, -sine_table], 1), np.concatenate([sine_table, cosine], 1)], 0
    )
    return forward.astype(jnp.bfloat16)


def band_response(band, length, band_count):
    mode_index = jnp.arange(length, dtype=jnp.int32)
    signed_modes = (mode_index - length * (mode_index >= length // 2).astype(jnp.int32)).astype(
        jnp.float32
    )
    center = (band.astype(jnp.float32) - (band_count - 1) / 2.0) * (length / (4.0 * band_count))
    band_width = length / 32.0
    offset_ratio = (signed_modes[None, :] - center[:, None]) / band_width
    single = (0.15 + 0.85 / (1.0 + offset_ratio**4)) / length
    return jnp.concatenate([single, single], 1)


def make_basis(channels, modes):
    channel_index = np.arange(channels, dtype=np.int32)
    order_index = np.arange(modes, dtype=np.int32)
    phase_index = order_index[None, :] * (2 * channel_index[:, None] + 1) % (4 * channels)
    return np.cos(phase_index.astype(np.float32) * np.float32(math.pi / (2 * channels))).astype(
        jnp.bfloat16
    )


NT = (((1,), (1,)), ((), ()))
BIG = 48 * 1024 * 1024


def dot32(left, right):
    return jnp.dot(left, right, preferred_element_type=jnp.float32)


def halves(value):
    high = value.astype(jnp.bfloat16)
    return high, (value - high.astype(jnp.float32)).astype(jnp.bfloat16)


def dot_split(left, right):
    left_high, left_low = left
    right_high, right_low = right
    return dot32(left_high, right_high) + (
        dot32(left_high, right_low) + dot32(left_low, right_high)
    )


def filter_kernel(shards, chunks, vis_ref, fwd_ref, inv_ref, resp_ref, weight_ref, basis_ref,
                  fringe_ref, proj_ref):
    batch, half = vis_ref.shape[0], vis_ref.shape[3]
    spectra = [
        dot32(vis_ref[i, :, 0, :], fwd_ref[:half]) + dot32(vis_ref[i, :, 1, :], fwd_ref[half:])
        for i in range(batch)
    ]
    spectra = [(spectra[i] * resp_ref[i]).astype(jnp.bfloat16) for i in range(batch)]
    for i in range(batch):
        fringe = lax.dot_general(inv_ref[...], spectra[i], NT, preferred_element_type=jnp.float32)
        fringe = (fringe * weight_ref[i]).astype(jnp.bfloat16)
        fringe_ref[i] = fringe
        projected = dot32(fringe, basis_ref[...])
        size = projected.shape[0] // chunks
        for h in range(chunks):
            piece = projected[h * size:(h + 1) * size].reshape(shards, -1, projected.shape[1])
            proj_ref[:, i, h] = piece.astype(jnp.bfloat16)


def inverse_kernel(batch, ridge, scales, start, weight_ref, basis_ref, basis_t_ref, out_ref):
    modes = out_ref.shape[1]
    eye = (
        lax.broadcasted_iota(jnp.int32, (modes, modes), 0)
        == lax.broadcasted_iota(jnp.int32, (modes, modes), 1)
    ).astype(jnp.float32)
    normals = [
        dot32(basis_t_ref[...] * weight_ref[i], basis_ref[...]) + ridge * eye for i in range(batch)
    ]
    first = scales[0]
    guess = [first * (2.0 * start * eye - start * start * normal) for normal in normals]
    normals = [halves(normal) for normal in normals]
    for scale in scales[1:]:
        guess_parts = [halves(value) for value in guess]
        product = [dot_split(n, g) for n, g in zip(normals, guess_parts)]
        change = [halves(2.0 * eye - value) for value in product]
        guess = [scale * dot_split(g, c) for g, c in zip(guess_parts, change)]
    for i in range(batch):
        out_ref[i] = guess[i]


def solve_kernel(batch, recv_ref, inverse_ref, *out_refs):
    for i in range(batch):
        inverse = halves(inverse_ref[i])
        for h, out_ref in enumerate(out_refs):
            total = jnp.sum(recv_ref[:, i, h].astype(jnp.float32), axis=0)
            out_ref[i] = dot_split(halves(total), inverse).astype(jnp.bfloat16)


def clean_kernel(ids_ref, fringe_ref, coef_ref, basis_t_ref, weight_ref, out_ref, total_ref):
    item = pl.program_id(0)

    @pl.when(item == 0)
    def _():
        total_ref[...] = jnp.zeros_like(total_ref)

    batch, size = fringe_ref.shape[0], fringe_ref.shape[1]
    for i in range(batch):
        coef = coef_ref[:, i].astype(jnp.float32)
        coef = coef.reshape(-1, coef.shape[2]).astype(jnp.bfloat16)
        fitted = dot32(coef, basis_t_ref[...]) * weight_ref[i]
        group = ids_ref[item * batch + i]
        total_ref[group, :size] += fringe_ref[i].astype(jnp.float32) - fitted
        total_ref[group, size:] += jnp.ones_like(total_ref[group, size:])

    @pl.when(item == pl.num_programs(0) - 1)
    def _():
        out_ref[...] = total_ref[...].astype(jnp.bfloat16)


def newton_scales(low, high):
    scales = []
    value = (high + low) / (high - low)
    while True:
        doubled = 2.0 * value * value
        scales.append(doubled / (doubled - 1.0))
        value = doubled - 1.0
        if value > 1e6:
            return scales


def full(shape):
    return pl.BlockSpec(shape, lambda i, *rest: (0,) * len(shape))


def lead(shape):
    return pl.BlockSpec(shape, lambda i, *rest: (i,) + (0,) * (len(shape) - 1))


def second(shape):
    return pl.BlockSpec(shape, lambda i, *rest: (0, i) + (0,) * (len(shape) - 2))


def per_device(vis, flags, band, group_id):
    items, chan, _, length = vis.shape
    both = 2 * length
    shards = lax.axis_size("freq")
    owners = lax.axis_size("bl")
    groups = GPO * owners
    time_local = length // shards
    rows = 2 * time_local
    pair = 2 if items % 2 == 0 else 1
    chunks = 2 if rows % 32 == 0 else 1
    rows //= chunks
    size = both // chunks
    bf16, f32 = jnp.bfloat16, jnp.float32

    table = fourier_tables(length)
    forward = jnp.asarray(table)
    inverse_t = forward
    if chunks == 1:
        inverse_t = table.reshape(2, shards, time_local, both)
        inverse_t = jnp.asarray(np.transpose(inverse_t, (1, 0, 2, 3)).reshape(both, both))
    response = band_response(band, length, NBAND).reshape(items, 1, both)
    basis = make_basis(CH, DELAYS)
    basis_t = jnp.asarray(basis.T.copy())
    basis = jnp.asarray(basis)
    basis_local = lax.dynamic_slice_in_dim(basis, lax.axis_index("freq") * chan, chan, 0)
    weight = 1.0 - flags.astype(f32)
    weight_rows = weight.reshape(items, 1, chan)
    weight_half = weight.astype(bf16)
    if shards <= 8:
        pieces = [weight_half] + [
            lax.ppermute(weight_half, "freq", [(d, (d - j) % shards) for d in range(shards)])
            for j in range(1, shards)
        ]
        doubled = jnp.concatenate(pieces + pieces, axis=1)
        offset = (shards - lax.axis_index("freq")) % shards * chan
        weight_full = lax.dynamic_slice_in_dim(doubled, offset, CH, 1)
    else:
        weight_full = lax.all_gather(weight_half, "freq", axis=1, tiled=True)
        response, weight_full = lax.optimization_barrier((response, weight_full))
    weight_full = weight_full.reshape(items, 1, CH)

    fringe, projected = pl.pallas_call(
        functools.partial(filter_kernel, shards, chunks),
        grid=(items // pair,),
        in_specs=[
            lead((pair, chan, 2, length)), full((both, both)), full((both, both)),
            lead((pair, 1, both)), lead((pair, 1, chan)), full((chan, DELAYS)),
        ],
        out_specs=[lead((pair, both, chan)), second((shards, pair, chunks, rows, DELAYS))],
        out_shape=[
            jax.ShapeDtypeStruct((items, both, chan), bf16),
            jax.ShapeDtypeStruct((shards, items, chunks, rows, DELAYS), bf16),
        ],
        compiler_params=pltpu.CompilerParams(vmem_limit_bytes=BIG),
        cost_estimate=pl.CostEstimate(
            flops=4 * items * chan * both * both, bytes_accessed=4 * items * chan * both,
            transcendentals=0,
        ),
    )(vis, forward, inverse_t, response, weight_rows, basis_local)

    projected, weight_full = lax.optimization_barrier((projected, weight_full))
    ridge = CH / 64.0
    high = ridge + 1.05 * CH
    batch = 4 if items % 4 == 0 else 1
    inverse = pl.pallas_call(
        functools.partial(
            inverse_kernel, batch, ridge, newton_scales(ridge, high), 2.0 / (ridge + high)
        ),
        grid=(items // batch,),
        in_specs=[lead((batch, 1, CH)), full((CH, DELAYS)), full((DELAYS, CH))],
        out_specs=lead((batch, DELAYS, DELAYS)),
        out_shape=jax.ShapeDtypeStruct((items, DELAYS, DELAYS), f32),
        compiler_params=pltpu.CompilerParams(vmem_limit_bytes=BIG),
        cost_estimate=pl.CostEstimate(
            flops=20_000_000_000, bytes_accessed=4 * items * DELAYS * DELAYS, transcendentals=0
        ),
    )(weight_full, basis, basis_t)

    received = lax.all_to_all(projected, "freq", split_axis=0, concat_axis=0, tiled=True)
    coefficients = pl.pallas_call(
        functools.partial(solve_kernel, batch),
        grid=(items // batch,),
        in_specs=[
            second((shards, batch, chunks, rows, DELAYS)), lead((batch, DELAYS, DELAYS)),
        ],
        out_specs=[lead((batch, rows, DELAYS))] * chunks,
        out_shape=[jax.ShapeDtypeStruct((items, rows, DELAYS), bf16)] * chunks,
        compiler_params=pltpu.CompilerParams(vmem_limit_bytes=BIG),
    )(received, inverse)
    basis_local_t = basis_local.T
    tall = size + 16

    def clean(h, gathered):
        return pl.pallas_call(
            clean_kernel,
            grid_spec=pltpu.PrefetchScalarGridSpec(
                num_scalar_prefetch=1,
                grid=(items // batch,),
                in_specs=[
                    pl.BlockSpec((batch, size, chan), lambda i, ids: (i, h, 0)),
                    second((shards, batch, rows, DELAYS)), full((DELAYS, chan)),
                    lead((batch, 1, chan)),
                ],
                out_specs=full((groups, tall, chan)),
                scratch_shapes=[pltpu.VMEM((groups, tall, chan), f32)],
            ),
            out_shape=jax.ShapeDtypeStruct((groups, tall, chan), bf16),
            compiler_params=pltpu.CompilerParams(vmem_limit_bytes=BIG),
            cost_estimate=pl.CostEstimate(
                flops=2_000_000_000, bytes_accessed=4 * items * size * chan, transcendentals=0
            ),
        )(group_id, fringe, gathered, basis_local_t, weight_rows)

    gathered = [lax.all_gather(part, "freq") for part in coefficients]
    pieces = []
    for h in range(chunks):
        sums = clean(h, gathered[h])
        arrived = lax.all_to_all(sums, "bl", split_axis=0, concat_axis=0, tiled=True)
        total = jnp.sum(arrived.reshape(owners, GPO, tall, chan).astype(f32), 0)
        counts = jnp.maximum(total[:, size:size + 1, :1], 1.0)
        mean = (total[:, :size] / counts).astype(bf16).reshape(GPO, shards, rows, chan)
        pieces.append(jnp.transpose(mean, (1, 0, 2, 3)))
    means = jnp.stack(pieces, 1)
    swapped = lax.all_to_all(means, "freq", split_axis=0, concat_axis=0, tiled=True)
    averaged = jnp.transpose(swapped, (2, 1, 3, 0, 4))
    return averaged.reshape(GPO, 2, time_local, CH)


def solution(mesh):
    in_specs = (P("bl", "freq", None, "win"), P("bl", "freq"), P("bl"), P("bl"))
    out_specs = P("bl", None, ("win", "freq"), None)
    return jax.shard_map(
        per_device, mesh=mesh, in_specs=in_specs, out_specs=out_specs, check_vma=False
    )
```

```python
import functools
import math

import jax
import jax.numpy as jnp
import numpy as np
from jax import lax
from jax.experimental import pallas as pl
from jax.experimental.pallas import tpu as pltpu
from jax.sharding import PartitionSpec as P

CH = 1536
DELAYS = 128
NBAND = 8
GPO = 2
CAP = 8


def fourier_tables(length):
    sample_index = np.arange(length, dtype=np.int32)
    phase_index = sample_index[:, None] * sample_index[None, :] % length
    angles = phase_index.astype(np.float32) * np.float32(2.0 * math.pi / length)
    cosine = np.cos(angles)
    sine_table = np.sin(angles)
    forward = np.concatenate(
        [np.concatenate([cosine, -sine_table], 1), np.concatenate([sine_table, cosine], 1)], 0
    )
    return forward.astype(jnp.bfloat16)


def band_response(band, length, band_count):
    mode_index = jnp.arange(length, dtype=jnp.int32)
    signed_modes = (mode_index - length * (mode_index >= length // 2).astype(jnp.int32)).astype(
        jnp.float32
    )
    center = (band.astype(jnp.float32) - (band_count - 1) / 2.0) * (length / (4.0 * band_count))
    band_width = length / 32.0
    offset_ratio = (signed_modes[None, :] - center[:, None]) / band_width
    single = (0.15 + 0.85 / (1.0 + offset_ratio**4)) / length
    return jnp.concatenate([single, single], 1)


def make_basis(channels, modes):
    channel_index = np.arange(channels, dtype=np.int32)
    order_index = np.arange(modes, dtype=np.int32)
    phase_index = order_index[None, :] * (2 * channel_index[:, None] + 1) % (4 * channels)
    return np.cos(phase_index.astype(np.float32) * np.float32(math.pi / (2 * channels))).astype(
        jnp.bfloat16
    )


NT = (((1,), (1,)), ((), ()))
BIG = 48 * 1024 * 1024


def dot32(left, right):
    return jnp.dot(left, right, preferred_element_type=jnp.float32)


def halves(value):
    high = value.astype(jnp.bfloat16)
    return high, (value - high.astype(jnp.float32)).astype(jnp.bfloat16)


def dot_split(left, right):
    left_high, left_low = left
    right_high, right_low = right
    return dot32(left_high, right_high) + (
        dot32(left_high, right_low) + dot32(left_low, right_high)
    )


def filter_kernel(shards, chunks, vis_ref, fwd_ref, inv_ref, resp_ref, weight_ref, basis_ref,
                  fringe_ref, proj_ref):
    batch, half = vis_ref.shape[0], vis_ref.shape[3]
    spectra = [
        dot32(vis_ref[i, :, 0, :], fwd_ref[:half]) + dot32(vis_ref[i, :, 1, :], fwd_ref[half:])
        for i in range(batch)
    ]
    spectra = [(spectra[i] * resp_ref[i]).astype(jnp.bfloat16) for i in range(batch)]
    for i in range(batch):
        fringe = lax.dot_general(inv_ref[...], spectra[i], NT, preferred_element_type=jnp.float32)
        fringe = (fringe * weight_ref[i]).astype(jnp.bfloat16)
        fringe_ref[i] = fringe
        projected = dot32(fringe, basis_ref[...])
        size = projected.shape[0] // chunks
        for h in range(chunks):
            piece = projected[h * size:(h + 1) * size].reshape(shards, -1, projected.shape[1])
            proj_ref[:, i, h] = piece.astype(jnp.bfloat16)


def inverse_kernel(batch, ridge, scales, start, weight_ref, basis_ref, basis_t_ref, out_ref):
    modes = out_ref.shape[1]
    eye = (
        lax.broadcasted_iota(jnp.int32, (modes, modes), 0)
        == lax.broadcasted_iota(jnp.int32, (modes, modes), 1)
    ).astype(jnp.float32)
    normals = [
        dot32(basis_t_ref[...] * weight_ref[i], basis_ref[...]) + ridge * eye for i in range(batch)
    ]
    first = scales[0]
    guess = [first * (2.0 * start * eye - start * start * normal) for normal in normals]
    normals = [halves(normal) for normal in normals]
    for scale in scales[1:]:
        guess_parts = [halves(value) for value in guess]
        product = [dot_split(n, g) for n, g in zip(normals, guess_parts)]
        change = [halves(2.0 * eye - value) for value in product]
        guess = [scale * dot_split(g, c) for g, c in zip(guess_parts, change)]
    for i in range(batch):
        out_ref[i] = guess[i]


def solve_kernel(batch, recv_ref, inverse_ref, *out_refs):
    for i in range(batch):
        inverse = halves(inverse_ref[i])
        for h, out_ref in enumerate(out_refs):
            total = jnp.sum(recv_ref[:, i, h].astype(jnp.float32), axis=0)
            out_ref[0, i] = dot_split(halves(total), inverse).astype(jnp.bfloat16)


def chain_kernel(shards, chunks, own_ref, out_ref, send_sem, recv_sem):
    me = lax.axis_index("freq")
    has_right, has_left = me < shards - 1, me > 0
    barrier = pltpu.get_barrier_semaphore()

    def greet(has, step):
        @pl.when(has)
        def _():
            pl.semaphore_signal(
                barrier, inc=1, device_id={"freq": me + step},
                device_id_type=pl.DeviceIdType.MESH,
            )

    greet(has_right, 1)
    greet(has_left, -1)
    pl.semaphore_wait(barrier, has_right.astype(jnp.int32) + has_left.astype(jnp.int32))

    def copy(way, h, hop, step):
        source = me - step * hop
        start = own_ref.at[h] if hop == 0 else out_ref.at[h, source]
        return pltpu.make_async_remote_copy(
            src_ref=start,
            dst_ref=out_ref.at[h, source],
            send_sem=send_sem.at[way, h, hop],
            recv_sem=recv_sem.at[way, h, hop],
            device_id={"freq": me + step},
            device_id_type=pl.DeviceIdType.MESH,
        )

    def arrival(way, h, hop, step):
        source = me - step * (hop + 1)
        return pltpu.make_async_remote_copy(
            src_ref=own_ref.at[h],
            dst_ref=out_ref.at[h, source],
            send_sem=send_sem.at[way, h, hop],
            recv_sem=recv_sem.at[way, h, hop],
            device_id={"freq": me - step},
            device_id_type=pl.DeviceIdType.MESH,
        )

    ways = ((0, 1, has_right), (1, -1, has_left))
    for hop in range(shards):
        for h in range(chunks):
            for way, step, has in ways:
                source = me - step * hop
                held = jnp.logical_and(source >= 0, source <= shards - 1)
                if hop > 0:
                    @pl.when(held)
                    def _():
                        arrival(way, h, hop - 1, step).wait_recv()
                if hop < shards - 1:
                    @pl.when(jnp.logical_and(held, has))
                    def _():
                        copy(way, h, hop, step).start()
        if hop == 0:
            for h in range(chunks):
                out_ref[h, me] = own_ref[h]
    for hop in range(shards - 1):
        for h in range(chunks):
            for way, step, has in ways:
                source = me - step * hop
                held = jnp.logical_and(source >= 0, source <= shards - 1)

                @pl.when(jnp.logical_and(held, has))
                def _():
                    copy(way, h, hop, step).wait_send()


def gather_chain(part, shards, chunks, call):
    if shards > 8:
        return jnp.stack([lax.all_gather(part[h], "freq") for h in range(chunks)])
    hops = max(shards - 1, 1)
    return pl.pallas_call(
        functools.partial(chain_kernel, shards, chunks),
        in_specs=[pl.BlockSpec(memory_space=pltpu.VMEM)],
        out_specs=pl.BlockSpec(memory_space=pltpu.VMEM),
        out_shape=jax.ShapeDtypeStruct((chunks, shards) + part.shape[1:], part.dtype),
        scratch_shapes=[
            pltpu.SemaphoreType.DMA((2, chunks, hops)),
            pltpu.SemaphoreType.DMA((2, chunks, hops)),
        ],
        compiler_params=pltpu.CompilerParams(
            collective_id=call, has_side_effects=True, vmem_limit_bytes=BIG
        ),
        cost_estimate=pl.CostEstimate(
            flops=20_000_000_000, bytes_accessed=2 * shards * part.size, transcendentals=0
        ),
    )(part)


def clean_kernel(ids_ref, fringe_ref, coef_ref, basis_t_ref, weight_ref, out_ref, total_ref):
    item = pl.program_id(0)

    @pl.when(item == 0)
    def _():
        total_ref[...] = jnp.zeros_like(total_ref)

    batch, size = fringe_ref.shape[0], fringe_ref.shape[1]
    for i in range(batch):
        coef = coef_ref[0, :, i].astype(jnp.float32)
        coef = coef.reshape(-1, coef.shape[2]).astype(jnp.bfloat16)
        fitted = dot32(coef, basis_t_ref[...]) * weight_ref[i]
        group = ids_ref[item * batch + i]
        total_ref[group, :size] += fringe_ref[i].astype(jnp.float32) - fitted
        total_ref[group, size:] += jnp.ones_like(total_ref[group, size:])

    @pl.when(item == pl.num_programs(0) - 1)
    def _():
        out_ref[...] = total_ref[...].astype(jnp.bfloat16)


def newton_scales(low, high):
    scales = []
    value = (high + low) / (high - low)
    while True:
        doubled = 2.0 * value * value
        scales.append(doubled / (doubled - 1.0))
        value = doubled - 1.0
        if value > 1e6:
            return scales


def full(shape):
    return pl.BlockSpec(shape, lambda i, *rest: (0,) * len(shape))


def lead(shape):
    return pl.BlockSpec(shape, lambda i, *rest: (i,) + (0,) * (len(shape) - 1))


def second(shape):
    return pl.BlockSpec(shape, lambda i, *rest: (0, i) + (0,) * (len(shape) - 2))


def per_device(vis, flags, band, group_id):
    items, chan, _, length = vis.shape
    both = 2 * length
    shards = lax.axis_size("freq")
    owners = lax.axis_size("bl")
    groups = GPO * owners
    time_local = length // shards
    rows = 2 * time_local
    pair = 2 if items % 2 == 0 else 1
    chunks = 2 if rows % 32 == 0 else 1
    rows //= chunks
    size = both // chunks
    bf16, f32 = jnp.bfloat16, jnp.float32

    table = fourier_tables(length)
    forward = jnp.asarray(table)
    inverse_t = forward
    if chunks == 1:
        inverse_t = table.reshape(2, shards, time_local, both)
        inverse_t = jnp.asarray(np.transpose(inverse_t, (1, 0, 2, 3)).reshape(both, both))
    response = band_response(band, length, NBAND).reshape(items, 1, both)
    basis = make_basis(CH, DELAYS)
    basis_t = jnp.asarray(basis.T.copy())
    basis = jnp.asarray(basis)
    basis_local = lax.dynamic_slice_in_dim(basis, lax.axis_index("freq") * chan, chan, 0)
    weight = 1.0 - flags.astype(f32)
    weight_rows = weight.reshape(items, 1, chan)
    weight_half = weight.astype(bf16)
    if shards <= 8:
        pieces = [weight_half] + [
            lax.ppermute(weight_half, "freq", [(d, (d - j) % shards) for d in range(shards)])
            for j in range(1, shards)
        ]
        doubled = jnp.concatenate(pieces + pieces, axis=1)
        offset = (shards - lax.axis_index("freq")) % shards * chan
        weight_full = lax.dynamic_slice_in_dim(doubled, offset, CH, 1)
    else:
        weight_full = lax.all_gather(weight_half, "freq", axis=1, tiled=True)
        response, weight_full = lax.optimization_barrier((response, weight_full))
    weight_full = weight_full.reshape(items, 1, CH)

    fringe, projected = pl.pallas_call(
        functools.partial(filter_kernel, shards, chunks),
        grid=(items // pair,),
        in_specs=[
            lead((pair, chan, 2, length)), full((both, both)), full((both, both)),
            lead((pair, 1, both)), lead((pair, 1, chan)), full((chan, DELAYS)),
        ],
        out_specs=[lead((pair, both, chan)), second((shards, pair, chunks, rows, DELAYS))],
        out_shape=[
            jax.ShapeDtypeStruct((items, both, chan), bf16),
            jax.ShapeDtypeStruct((shards, items, chunks, rows, DELAYS), bf16),
        ],
        compiler_params=pltpu.CompilerParams(vmem_limit_bytes=BIG),
        cost_estimate=pl.CostEstimate(
            flops=4 * items * chan * both * both, bytes_accessed=4 * items * chan * both,
            transcendentals=0,
        ),
    )(vis, forward, inverse_t, response, weight_rows, basis_local)

    projected, weight_full = lax.optimization_barrier((projected, weight_full))
    ridge = CH / 64.0
    high = ridge + 1.05 * CH
    batch = 4 if items % 4 == 0 else 1
    inverse = pl.pallas_call(
        functools.partial(
            inverse_kernel, batch, ridge, newton_scales(ridge, high), 2.0 / (ridge + high)
        ),
        grid=(items // batch,),
        in_specs=[lead((batch, 1, CH)), full((CH, DELAYS)), full((DELAYS, CH))],
        out_specs=lead((batch, DELAYS, DELAYS)),
        out_shape=jax.ShapeDtypeStruct((items, DELAYS, DELAYS), f32),
        compiler_params=pltpu.CompilerParams(vmem_limit_bytes=BIG),
        cost_estimate=pl.CostEstimate(
            flops=20_000_000_000, bytes_accessed=4 * items * DELAYS * DELAYS, transcendentals=0
        ),
    )(weight_full, basis, basis_t)

    received = lax.all_to_all(projected, "freq", split_axis=0, concat_axis=0, tiled=True)
    coefficients = pl.pallas_call(
        functools.partial(solve_kernel, batch),
        grid=(items // batch,),
        in_specs=[
            second((shards, batch, chunks, rows, DELAYS)), lead((batch, DELAYS, DELAYS)),
        ],
        out_specs=[second((1, batch, rows, DELAYS))] * chunks,
        out_shape=[jax.ShapeDtypeStruct((1, items, rows, DELAYS), bf16)] * chunks,
        compiler_params=pltpu.CompilerParams(vmem_limit_bytes=BIG),
    )(received, inverse)
    basis_local_t = basis_local.T
    tall = size + 16

    def clean(h, gathered):
        return pl.pallas_call(
            clean_kernel,
            grid_spec=pltpu.PrefetchScalarGridSpec(
                num_scalar_prefetch=1,
                grid=(items // batch,),
                in_specs=[
                    pl.BlockSpec((batch, size, chan), lambda i, ids: (i, h, 0)),
                    pl.BlockSpec((1, shards, batch, rows, DELAYS), lambda i, ids: (0, 0, i, 0, 0)),
                    full((DELAYS, chan)),
                    lead((batch, 1, chan)),
                ],
                out_specs=full((groups, tall, chan)),
                scratch_shapes=[pltpu.VMEM((groups, tall, chan), f32)],
            ),
            out_shape=jax.ShapeDtypeStruct((groups, tall, chan), bf16),
            compiler_params=pltpu.CompilerParams(vmem_limit_bytes=BIG),
            cost_estimate=pl.CostEstimate(
                flops=2_000_000_000, bytes_accessed=4 * items * size * chan, transcendentals=0
            ),
        )(group_id, fringe, gathered, basis_local_t, weight_rows)

    pieces = []
    for h in range(chunks):
        part = coefficients[h]
        if h:
            part, sums = lax.optimization_barrier((part, sums))
        sums = clean(h, gather_chain(part, shards, 1, h))
        arrived = lax.all_to_all(sums, "bl", split_axis=0, concat_axis=0, tiled=True)
        total = jnp.sum(arrived.reshape(owners, GPO, tall, chan).astype(f32), 0)
        counts = jnp.maximum(total[:, size:size + 1, :1], 1.0)
        mean = (total[:, :size] / counts).astype(bf16).reshape(GPO, shards, rows, chan)
        pieces.append(jnp.transpose(mean, (1, 0, 2, 3)))
    means = jnp.stack(pieces, 1)
    swapped = lax.all_to_all(means, "freq", split_axis=0, concat_axis=0, tiled=True)
    averaged = jnp.transpose(swapped, (2, 1, 3, 0, 4))
    return averaged.reshape(GPO, 2, time_local, CH)


def solution(mesh):
    in_specs = (P("bl", "freq", None, "win"), P("bl", "freq"), P("bl"), P("bl"))
    out_specs = P("bl", None, ("win", "freq"), None)
    return jax.shard_map(
        per_device, mesh=mesh, in_specs=in_specs, out_specs=out_specs, check_vma=False
    )
```

```python
import functools
import math

import jax
import jax.numpy as jnp
import numpy as np
from jax import lax
from jax.experimental import pallas as pl
from jax.experimental.pallas import tpu as pltpu
from jax.sharding import PartitionSpec as P

CH = 1536
DELAYS = 128
NBAND = 8
GPO = 2
CAP = 8


def fourier_tables(length):
    sample_index = np.arange(length, dtype=np.int32)
    phase_index = sample_index[:, None] * sample_index[None, :] % length
    angles = phase_index.astype(np.float32) * np.float32(2.0 * math.pi / length)
    cosine = np.cos(angles)
    sine_table = np.sin(angles)
    forward = np.concatenate(
        [np.concatenate([cosine, -sine_table], 1), np.concatenate([sine_table, cosine], 1)], 0
    )
    return forward.astype(jnp.bfloat16)


def band_response(band, length, band_count):
    mode_index = jnp.arange(length, dtype=jnp.int32)
    signed_modes = (mode_index - length * (mode_index >= length // 2).astype(jnp.int32)).astype(
        jnp.float32
    )
    center = (band.astype(jnp.float32) - (band_count - 1) / 2.0) * (length / (4.0 * band_count))
    band_width = length / 32.0
    offset_ratio = (signed_modes[None, :] - center[:, None]) / band_width
    single = (0.15 + 0.85 / (1.0 + offset_ratio**4)) / length
    return jnp.concatenate([single, single], 1)


def make_basis(channels, modes):
    channel_index = np.arange(channels, dtype=np.int32)
    order_index = np.arange(modes, dtype=np.int32)
    phase_index = order_index[None, :] * (2 * channel_index[:, None] + 1) % (4 * channels)
    return np.cos(phase_index.astype(np.float32) * np.float32(math.pi / (2 * channels))).astype(
        jnp.bfloat16
    )


NT = (((1,), (1,)), ((), ()))
BIG = 48 * 1024 * 1024


def dot32(left, right):
    return jnp.dot(left, right, preferred_element_type=jnp.float32)


def halves(value):
    high = value.astype(jnp.bfloat16)
    return high, (value - high.astype(jnp.float32)).astype(jnp.bfloat16)


def dot_split(left, right):
    left_high, left_low = left
    right_high, right_low = right
    return dot32(left_high, right_high) + (
        dot32(left_high, right_low) + dot32(left_low, right_high)
    )


def filter_kernel(shards, chunks, vis_ref, fwd_ref, inv_ref, resp_ref, weight_ref, basis_ref,
                  fringe_ref, proj_ref):
    batch, half = vis_ref.shape[0], vis_ref.shape[3]
    spectra = [
        dot32(vis_ref[i, :, 0, :], fwd_ref[:half]) + dot32(vis_ref[i, :, 1, :], fwd_ref[half:])
        for i in range(batch)
    ]
    spectra = [(spectra[i] * resp_ref[i]).astype(jnp.bfloat16) for i in range(batch)]
    for i in range(batch):
        fringe = lax.dot_general(inv_ref[...], spectra[i], NT, preferred_element_type=jnp.float32)
        fringe = (fringe * weight_ref[i]).astype(jnp.bfloat16)
        fringe_ref[i] = fringe
        projected = dot32(fringe, basis_ref[...])
        size = projected.shape[0] // chunks
        for h in range(chunks):
            piece = projected[h * size:(h + 1) * size].reshape(shards, -1, projected.shape[1])
            proj_ref[:, i, h] = piece.astype(jnp.bfloat16)


def inverse_kernel(batch, ridge, scales, start, weight_ref, basis_ref, basis_t_ref, out_ref):
    modes = out_ref.shape[1]
    eye = (
        lax.broadcasted_iota(jnp.int32, (modes, modes), 0)
        == lax.broadcasted_iota(jnp.int32, (modes, modes), 1)
    ).astype(jnp.float32)
    normals = [
        dot32(basis_t_ref[...] * weight_ref[i], basis_ref[...]) + ridge * eye for i in range(batch)
    ]
    first = scales[0]
    guess = [first * (2.0 * start * eye - start * start * normal) for normal in normals]
    normals = [halves(normal) for normal in normals]
    for scale in scales[1:]:
        guess_parts = [halves(value) for value in guess]
        product = [dot_split(n, g) for n, g in zip(normals, guess_parts)]
        change = [halves(2.0 * eye - value) for value in product]
        guess = [scale * dot_split(g, c) for g, c in zip(guess_parts, change)]
    for i in range(batch):
        out_ref[i] = guess[i]


def solve_kernel(batch, recv_ref, inverse_ref, *out_refs):
    for i in range(batch):
        inverse = halves(inverse_ref[i])
        for h, out_ref in enumerate(out_refs):
            total = jnp.sum(recv_ref[:, i, h].astype(jnp.float32), axis=0)
            out_ref[0, i] = dot_split(halves(total), inverse).astype(jnp.bfloat16)


def chain_kernel(shards, chunks, own_ref, out_ref, send_sem, recv_sem):
    me = lax.axis_index("freq")
    has_right, has_left = me < shards - 1, me > 0
    barrier = pltpu.get_barrier_semaphore()

    def greet(has, step):
        @pl.when(has)
        def _():
            pl.semaphore_signal(
                barrier, inc=1, device_id={"freq": me + step},
                device_id_type=pl.DeviceIdType.MESH,
            )

    greet(has_right, 1)
    greet(has_left, -1)
    pl.semaphore_wait(barrier, has_right.astype(jnp.int32) + has_left.astype(jnp.int32))

    def copy(way, h, hop, step):
        source = me - step * hop
        start = own_ref.at[h] if hop == 0 else out_ref.at[h, source]
        return pltpu.make_async_remote_copy(
            src_ref=start,
            dst_ref=out_ref.at[h, source],
            send_sem=send_sem.at[way, h, hop],
            recv_sem=recv_sem.at[way, h, hop],
            device_id={"freq": me + step},
            device_id_type=pl.DeviceIdType.MESH,
        )

    def arrival(way, h, hop, step):
        source = me - step * (hop + 1)
        return pltpu.make_async_remote_copy(
            src_ref=own_ref.at[h],
            dst_ref=out_ref.at[h, source],
            send_sem=send_sem.at[way, h, hop],
            recv_sem=recv_sem.at[way, h, hop],
            device_id={"freq": me - step},
            device_id_type=pl.DeviceIdType.MESH,
        )

    ways = ((0, 1, has_right), (1, -1, has_left))
    for hop in range(shards):
        for h in range(chunks):
            for way, step, has in ways:
                source = me - step * hop
                held = jnp.logical_and(source >= 0, source <= shards - 1)
                if hop > 0:
                    @pl.when(held)
                    def _():
                        arrival(way, h, hop - 1, step).wait_recv()
                if hop < shards - 1:
                    @pl.when(jnp.logical_and(held, has))
                    def _():
                        copy(way, h, hop, step).start()
        if hop == 0:
            for h in range(chunks):
                out_ref[h, me] = own_ref[h]
    for hop in range(shards - 1):
        for h in range(chunks):
            for way, step, has in ways:
                source = me - step * hop
                held = jnp.logical_and(source >= 0, source <= shards - 1)

                @pl.when(jnp.logical_and(held, has))
                def _():
                    copy(way, h, hop, step).wait_send()


def gather_chain(part, shards, chunks, call):
    if shards > 8:
        return jnp.stack([lax.all_gather(part[h], "freq") for h in range(chunks)])
    hops = max(shards - 1, 1)
    return pl.pallas_call(
        functools.partial(chain_kernel, shards, chunks),
        in_specs=[pl.BlockSpec(memory_space=pltpu.VMEM)],
        out_specs=pl.BlockSpec(memory_space=pltpu.VMEM),
        out_shape=jax.ShapeDtypeStruct((chunks, shards) + part.shape[1:], part.dtype),
        scratch_shapes=[
            pltpu.SemaphoreType.DMA((2, chunks, hops)),
            pltpu.SemaphoreType.DMA((2, chunks, hops)),
        ],
        compiler_params=pltpu.CompilerParams(
            collective_id=call, has_side_effects=True, vmem_limit_bytes=BIG
        ),
        cost_estimate=pl.CostEstimate(
            flops=20_000_000_000, bytes_accessed=2 * shards * part.size, transcendentals=0
        ),
    )(part)


def clean_kernel(ids_ref, fringe_ref, coef_ref, basis_t_ref, weight_ref, out_ref, total_ref):
    item = pl.program_id(0)

    @pl.when(item == 0)
    def _():
        total_ref[...] = jnp.zeros_like(total_ref)

    batch, size = fringe_ref.shape[0], fringe_ref.shape[1]
    for i in range(batch):
        coef = coef_ref[0, :, i].astype(jnp.float32)
        coef = coef.reshape(-1, coef.shape[2]).astype(jnp.bfloat16)
        fitted = dot32(coef, basis_t_ref[...]) * weight_ref[i]
        group = ids_ref[item * batch + i]
        total_ref[group, :size] += fringe_ref[i].astype(jnp.float32) - fitted
        total_ref[group, size:] += jnp.ones_like(total_ref[group, size:])

    @pl.when(item == pl.num_programs(0) - 1)
    def _():
        out_ref[...] = total_ref[...].astype(jnp.bfloat16)


def newton_scales(low, high):
    scales = []
    value = (high + low) / (high - low)
    while True:
        doubled = 2.0 * value * value
        scales.append(doubled / (doubled - 1.0))
        value = doubled - 1.0
        if value > 1e6:
            return scales


def full(shape):
    return pl.BlockSpec(shape, lambda i, *rest: (0,) * len(shape))


def lead(shape):
    return pl.BlockSpec(shape, lambda i, *rest: (i,) + (0,) * (len(shape) - 1))


def second(shape):
    return pl.BlockSpec(shape, lambda i, *rest: (0, i) + (0,) * (len(shape) - 2))


def per_device(vis, flags, band, group_id):
    items, chan, _, length = vis.shape
    both = 2 * length
    shards = lax.axis_size("freq")
    owners = lax.axis_size("bl")
    groups = GPO * owners
    time_local = length // shards
    rows = 2 * time_local
    pair = 2 if items % 2 == 0 else 1
    chunks = 2 if rows % 32 == 0 else 1
    rows //= chunks
    size = both // chunks
    bf16, f32 = jnp.bfloat16, jnp.float32

    table = fourier_tables(length)
    forward = jnp.asarray(table)
    inverse_t = forward
    if chunks == 1:
        inverse_t = table.reshape(2, shards, time_local, both)
        inverse_t = jnp.asarray(np.transpose(inverse_t, (1, 0, 2, 3)).reshape(both, both))
    response = band_response(band, length, NBAND).reshape(items, 1, both)
    basis = make_basis(CH, DELAYS)
    basis_t = jnp.asarray(basis.T.copy())
    basis = jnp.asarray(basis)
    basis_local = lax.dynamic_slice_in_dim(basis, lax.axis_index("freq") * chan, chan, 0)
    weight = 1.0 - flags.astype(f32)
    weight_rows = weight.reshape(items, 1, chan)
    weight_half = weight.astype(bf16)
    if shards <= 8:
        pieces = [weight_half] + [
            lax.ppermute(weight_half, "freq", [(d, (d - j) % shards) for d in range(shards)])
            for j in range(1, shards)
        ]
        doubled = jnp.concatenate(pieces + pieces, axis=1)
        offset = (shards - lax.axis_index("freq")) % shards * chan
        weight_full = lax.dynamic_slice_in_dim(doubled, offset, CH, 1)
    else:
        weight_full = lax.all_gather(weight_half, "freq", axis=1, tiled=True)
        response, weight_full = lax.optimization_barrier((response, weight_full))
    weight_full = weight_full.reshape(items, 1, CH)

    fringe, projected = pl.pallas_call(
        functools.partial(filter_kernel, shards, chunks),
        grid=(items // pair,),
        in_specs=[
            lead((pair, chan, 2, length)), full((both, both)), full((both, both)),
            lead((pair, 1, both)), lead((pair, 1, chan)), full((chan, DELAYS)),
        ],
        out_specs=[lead((pair, both, chan)), second((shards, pair, chunks, rows, DELAYS))],
        out_shape=[
            jax.ShapeDtypeStruct((items, both, chan), bf16),
            jax.ShapeDtypeStruct((shards, items, chunks, rows, DELAYS), bf16),
        ],
        compiler_params=pltpu.CompilerParams(vmem_limit_bytes=BIG),
        cost_estimate=pl.CostEstimate(
            flops=4 * items * chan * both * both, bytes_accessed=4 * items * chan * both,
            transcendentals=0,
        ),
    )(vis, forward, inverse_t, response, weight_rows, basis_local)

    projected, weight_full = lax.optimization_barrier((projected, weight_full))
    ridge = CH / 64.0
    high = ridge + 1.05 * CH
    batch = 4 if items % 4 == 0 else 1
    inverse = pl.pallas_call(
        functools.partial(
            inverse_kernel, batch, ridge, newton_scales(ridge, high), 2.0 / (ridge + high)
        ),
        grid=(items // batch,),
        in_specs=[lead((batch, 1, CH)), full((CH, DELAYS)), full((DELAYS, CH))],
        out_specs=lead((batch, DELAYS, DELAYS)),
        out_shape=jax.ShapeDtypeStruct((items, DELAYS, DELAYS), f32),
        compiler_params=pltpu.CompilerParams(vmem_limit_bytes=BIG),
        cost_estimate=pl.CostEstimate(
            flops=20_000_000_000, bytes_accessed=4 * items * DELAYS * DELAYS, transcendentals=0
        ),
    )(weight_full, basis, basis_t)

    received = lax.all_to_all(projected, "freq", split_axis=0, concat_axis=0, tiled=True)
    coefficients = pl.pallas_call(
        functools.partial(solve_kernel, batch),
        grid=(items // batch,),
        in_specs=[
            second((shards, batch, chunks, rows, DELAYS)), lead((batch, DELAYS, DELAYS)),
        ],
        out_specs=[second((1, batch, rows, DELAYS))] * chunks,
        out_shape=[jax.ShapeDtypeStruct((1, items, rows, DELAYS), bf16)] * chunks,
        compiler_params=pltpu.CompilerParams(vmem_limit_bytes=BIG),
    )(received, inverse)
    basis_local_t = basis_local.T
    tall = size + 16

    def clean(h, gathered):
        return pl.pallas_call(
            clean_kernel,
            grid_spec=pltpu.PrefetchScalarGridSpec(
                num_scalar_prefetch=1,
                grid=(items // batch,),
                in_specs=[
                    pl.BlockSpec((batch, size, chan), lambda i, ids: (i, h, 0)),
                    pl.BlockSpec((1, shards, batch, rows, DELAYS), lambda i, ids: (0, 0, i, 0, 0)),
                    full((DELAYS, chan)),
                    lead((batch, 1, chan)),
                ],
                out_specs=full((groups, tall, chan)),
                scratch_shapes=[pltpu.VMEM((groups, tall, chan), f32)],
            ),
            out_shape=jax.ShapeDtypeStruct((groups, tall, chan), bf16),
            compiler_params=pltpu.CompilerParams(vmem_limit_bytes=BIG),
            cost_estimate=pl.CostEstimate(
                flops=2_000_000_000, bytes_accessed=4 * items * size * chan, transcendentals=0
            ),
        )(group_id, fringe, gathered, basis_local_t, weight_rows)

    pieces = []
    for h in range(chunks):
        part = coefficients[h]
        if h:
            part, sums = lax.optimization_barrier((part, sums))
        sums = clean(h, gather_chain(part, shards, 1, h))
        if h:
            sums, pieces[-1] = lax.optimization_barrier((sums, pieces[-1]))
        arrived = lax.all_to_all(sums, "bl", split_axis=0, concat_axis=0, tiled=True)
        total = jnp.sum(arrived.reshape(owners, GPO, tall, chan).astype(f32), 0)
        counts = jnp.maximum(total[:, size:size + 1, :1], 1.0)
        mean = (total[:, :size] / counts).astype(bf16).reshape(GPO, shards, rows, chan)
        pieces.append(jnp.transpose(mean, (1, 0, 2, 3)))
    if shards > 8:
        swapped = [
            lax.all_to_all(piece, "freq", split_axis=0, concat_axis=0, tiled=True)
            for piece in pieces
        ]
        swapped = [jnp.concatenate(list(piece), axis=-1) for piece in swapped]
    else:
        me = lax.axis_index("freq")
        swapped = []
        for piece in pieces:
            parts = [lax.dynamic_index_in_dim(piece, me, 0, keepdims=False)]
            for j in range(1, shards):
                out = lax.dynamic_index_in_dim(piece, (me + shards - j) % shards, 0, keepdims=False)
                parts.append(
                    lax.ppermute(out, "freq", [(d, (d - j) % shards) for d in range(shards)])
                )
            doubled = jnp.concatenate(parts + parts, axis=-1)
            offset = (shards - me) % shards * chan
            swapped.append(lax.dynamic_slice_in_dim(doubled, offset, CH, 2))
    averaged = [piece.reshape(GPO, 2 // chunks, time_local, CH) for piece in swapped]
    return jnp.concatenate(averaged, 1)


def solution(mesh):
    in_specs = (P("bl", "freq", None, "win"), P("bl", "freq"), P("bl"), P("bl"))
    out_specs = P("bl", None, ("win", "freq"), None)
    return jax.shard_map(
        per_device, mesh=mesh, in_specs=in_specs, out_specs=out_specs, check_vma=False
    )
```
